32 devices in a mesh: rows: 8 (over z, x), heads: 4 (over y, core).
Axes of the slice: x: 2, y: 2, z: 4, core: 2. Of those that a mesh axis runs over, the one named last changes fastest.
Arguments:
- stream: bfloat16 [128, 4096], P('rows', 'heads'), may hold values from -6 to 6
- self_query: bfloat16 [128, 8192], P('rows', 'heads'), may hold values from -200 to 200
- new_kv: bfloat16 [128, 8, 256], P('rows', 'heads'), may hold values from -8 to 8
- cache_pool: bfloat16 [768, 64, 8, 256], P('rows', None, 'heads'), may hold values from -8 to 8
- page_table: int32 [128, 6], P('rows'), may hold values from 0 to 95, as said below
- lengths: int32 [128], P('rows'), may hold values from 1 to 383, as said below
- migration: int32 [128, 2], P('rows'), may hold values from -1 to 15, as said below
- image_of: int32 [128], replicated, may hold values from 0 to 7, as said below
- cross_query: bfloat16 [128, 8192], P('rows', 'heads'), may hold values from -200 to 200
- image_cache: bfloat16 [8, 1024, 8, 256], P(None, 'rows', 'heads'), may hold values from -8 to 8
- self_output: bfloat16 [8192, 4096], P('heads'), may hold values from -0.125 to 0.125
- cross_output: bfloat16 [8192, 4096], P('heads'), may hold values from -0.5 to 0.5
- cross_gate: float32 [1], replicated, may hold values from 0.3 to 1.2
Outputs:
- self_update: bfloat16 [128, 4096], P('rows', 'heads')
- cross_update: bfloat16 [128, 4096], P('rows', 'heads')
- new_cache: bfloat16 [128, 384, 8, 256], P('rows', None, 'heads')
The draws below stay inside these ranges and needn't reach their ends.
Inputs may be any that keep to these rules, and one draw needn't show every extreme that they name: `page_table`: each index of rows lists, over its 16 rows, every page number of its block of 96 pages exactly once. The new token of row r goes to position lengths[r]. `migration`: A finished row gives (-1, -1), a live row (destination index along rows, slot). No slot of a destination is named twice. The slots of a destination form aligned groups of 4, each group named only by rows of one index of rows; the rows of one index go to 4 different destinations, at most 4 rows to each, and some index sends 4 live rows to one destination. Some destination has all 16 slots named. `image_of`: every image is the image of exactly 16 rows.
All inputs are finite; a program needn't handle non-finite values.
Results may differ from the reference program's by a relative error of at most 0.0085.
Values may be sent and summed in bfloat16 or wider, within the bound.
A program may use at most 128 MiB of HBM per device.

```python
import math
import jax
import jax.numpy as jnp
from jax import lax

QH = 64
KVH = 8
HD = 128
DW = 4096
ROWS_DEV = 16
PG = 64
MAXPG = 6
GROUP = 16
ROWS = 128
HIST = 384
IMAGES = 8
IMG_TOK = 1024


def distinct_order(subkey, count_rows, count):
    scores = jax.random.randint(subkey, (count_rows, count), 0, 1 << 20) * count + jnp.arange(count, dtype=jnp.int32)[None, :]
    return jnp.argsort(scores, axis=1).astype(jnp.int32)


def offset_order(subkey, devices):
    steps = jnp.arange(devices, dtype=jnp.int32)
    scores = jax.random.randint(subkey, (devices,), 0, 1 << 20) * devices + steps
    scores = jnp.where(steps == devices // 2, -2, scores)
    scores = jnp.where(steps == devices - 1, -1, scores)
    return jnp.argsort(scores).astype(jnp.int32)


def layout(key):
    devices = ROWS // ROWS_DEV
    per_pair = max(2, 2 * ROWS_DEV // devices)
    groups = ROWS_DEV // per_pair
    pool_pages = ROWS_DEV * MAXPG
    page_table = distinct_order(jax.random.fold_in(key, 101), devices, pool_pages).reshape(ROWS, MAXPG)
    image_of = (distinct_order(jax.random.fold_in(key, 102), 1, ROWS)[0] // GROUP).astype(jnp.int32)
    offsets = offset_order(jax.random.fold_in(key, 103), devices)[:groups]
    order_rows = distinct_order(jax.random.fold_in(key, 104), devices, ROWS_DEV)
    inverse = jnp.argsort(order_rows, axis=1).astype(jnp.int32)
    source = jnp.arange(devices, dtype=jnp.int32)[:, None]
    target_dev = ((source - offsets[inverse // per_pair]) % devices).astype(jnp.int32)
    filled = jax.random.randint(jax.random.fold_in(key, 105), (devices,), 0, 4) == 0
    forced = jax.random.randint(jax.random.fold_in(key, 106), (), 0, devices)
    filled = filled | (jnp.arange(devices, dtype=jnp.int32) == forced)
    living = filled[target_dev] | (jax.random.randint(jax.random.fold_in(key, 107), (devices, ROWS_DEV), 0, 100) < 80)
    migration = jnp.stack([jnp.where(living, target_dev, -1), jnp.where(living, inverse, -1)], axis=-1).reshape(ROWS, 2).astype(jnp.int32)
    lengths = jax.random.randint(jax.random.fold_in(key, 108), (ROWS,), 1, HIST).astype(jnp.int32)
    return (page_table, image_of, migration, lengths)


def bounded_normal(subkey, shape_of, spread_factor):
    return jnp.clip(jax.random.normal(subkey, shape_of, jnp.float32), -6.0, 6.0) * spread_factor


def floats(key):
    self_query = bounded_normal(jax.random.fold_in(key, 201), (ROWS, QH, HD), 2.0)
    new_kv = bounded_normal(jax.random.fold_in(key, 202), (ROWS, KVH, 2 * HD), 1.0)
    cache_pool = bounded_normal(jax.random.fold_in(key, 203), (ROWS * MAXPG, PG, KVH, 2 * HD), 1.0)
    cross_query = bounded_normal(jax.random.fold_in(key, 204), (ROWS, QH, HD), 2.0)
    image_cache = bounded_normal(jax.random.fold_in(key, 205), (IMAGES, IMG_TOK, KVH, 2 * HD), 1.0)
    return (self_query.reshape(ROWS, QH * HD), new_kv, cache_pool, cross_query.reshape(ROWS, QH * HD), image_cache)


def draw_self_query(key, part):
    return floats(key)[0].astype(jnp.bfloat16)


def draw_new_kv(key, part):
    return floats(key)[1].astype(jnp.bfloat16)


def draw_cache_pool(key, part):
    return floats(key)[2].astype(jnp.bfloat16)


def draw_cross_query(key, part):
    return floats(key)[3].astype(jnp.bfloat16)


def draw_image_cache(key, part):
    return floats(key)[4].astype(jnp.bfloat16)


def draw_page_table(key, part):
    return layout(key)[0]


def draw_image_of(key, part):
    return layout(key)[1]


def draw_migration(key, part):
    return layout(key)[2]


def draw_lengths(key, part):
    return layout(key)[3]


def block_scale(stream_key, shape, pieces, low, top_value):
    gain = 1.0
    for axis_at, shards_of in pieces:
        draws = jax.random.uniform(jax.random.fold_in(jax.random.fold_in(stream_key, 6), axis_at), (shards_of,), jnp.float32, low / len(pieces), top_value / len(pieces))
        gain = gain * jnp.repeat(jnp.exp(draws), shape[axis_at] // shards_of).reshape((-1,) + (1,) * (len(shape) - 1 - axis_at))
    return gain


def centred(stream_key, dims, spread, limit, pieces=(), kind=jnp.bfloat16):
    entries = spread * jax.random.normal(stream_key, dims, jnp.float32)
    if pieces:
        entries = entries * block_scale(stream_key, dims, pieces, -0.22, 0.18)
    return jnp.clip(entries, -limit, limit).astype(kind)


def setup_inputs(seed: int = 0) -> dict:
    key_list = jax.random.split(jax.random.key(seed), 14)
    return {
        "stream": centred(key_list[0], (ROWS, DW), 1.0, 6.0, ((0, 8), (1, 4))),
        "self_query": draw_self_query(jax.random.fold_in(key_list[13], 71), 0),
        "new_kv": draw_new_kv(jax.random.fold_in(key_list[13], 71), 0),
        "cache_pool": draw_cache_pool(jax.random.fold_in(key_list[13], 71), 0),
        "page_table": draw_page_table(jax.random.fold_in(key_list[13], 71), 0),
        "lengths": draw_lengths(jax.random.fold_in(key_list[13], 71), 0),
        "migration": draw_migration(jax.random.fold_in(key_list[13], 71), 0),
        "image_of": draw_image_of(jax.random.fold_in(key_list[13], 71), 0),
        "cross_query": draw_cross_query(jax.random.fold_in(key_list[13], 71), 0),
        "image_cache": draw_image_cache(jax.random.fold_in(key_list[13], 71), 0),
        "self_output": centred(key_list[10], (QH * HD, DW), (QH * HD // 4) ** -0.5, 0.125, ((0, 4),)),
        "cross_output": centred(key_list[11], (QH * HD, DW), (QH * HD // 64) ** -0.5, 0.5, ((0, 4),)),
        "cross_gate": jnp.clip(jax.random.uniform(key_list[12], (1,), jnp.float32, 0.3, 1.2), 0.3, 1.2),
    }


def attend_row(queries, keys, values, visible):
    scores = jnp.einsum('kgd,tkd->kgt', queries, keys) * (1.0 / math.sqrt(HD))
    scores = jnp.where(visible[None, None, :], scores, -1e+30)
    highest = lax.optimization_barrier(jnp.max(scores, axis=-1, keepdims=True))
    weights = jnp.exp(scores - highest)
    weight_sum = lax.optimization_barrier(jnp.sum(weights, axis=-1))
    blended = jnp.einsum('kgt,tkd->kgd', weights, values)
    return (blended / weight_sum[..., None]).reshape(-1).astype(jnp.bfloat16)

def reference(stream, self_query, new_kv, cache_pool, page_table, lengths, migration, image_of, cross_query, image_cache, self_output, cross_output, cross_gate):
    group_size = QH // KVH
    device = jnp.arange(ROWS, dtype=jnp.int32) // ROWS_DEV
    page_index = (page_table + (device * (ROWS_DEV * MAXPG))[:, None]).astype(jnp.int32)
    taken = cache_pool[page_index.reshape(-1)].reshape(ROWS, HIST, KVH, 2 * HD)
    position = jnp.arange(HIST, dtype=jnp.int32)[None, :]
    written = jnp.where((position == lengths[:, None])[:, :, None, None], new_kv[:, None], taken)
    visible = position <= lengths[:, None]

    def self_one(element):
        query_row, rows_kv, visible_row = element
        grouped = query_row.astype(jnp.float32).reshape(KVH, group_size, HD)
        return attend_row(grouped, rows_kv[..., :HD].astype(jnp.float32), rows_kv[..., HD:].astype(jnp.float32), visible_row)
    self_attended = lax.map(self_one, (self_query, written, visible))
    everything = jnp.ones((IMG_TOK,), dtype=bool)

    def cross_one(element):
        query_row, image_id = element
        tokens = lax.dynamic_index_in_dim(image_cache, image_id, 0, keepdims=False)
        grouped = query_row.astype(jnp.float32).reshape(KVH, group_size, HD)
        return attend_row(grouped, tokens[..., :HD].astype(jnp.float32), tokens[..., HD:].astype(jnp.float32), everything)
    cross_attended = lax.map(cross_one, (cross_query, image_of))
    self_sum = jnp.dot(self_attended, self_output, preferred_element_type=jnp.float32)
    cross_sum = jnp.dot(cross_attended, cross_output, preferred_element_type=jnp.float32)
    self_rows = (stream.astype(jnp.float32) + self_sum).astype(jnp.bfloat16)
    cross_rows = (jnp.tanh(cross_gate[0]) * cross_sum).astype(jnp.bfloat16)
    target = jnp.where(migration[:, 0] >= 0, migration[:, 0] * ROWS_DEV + migration[:, 1], ROWS).astype(jnp.int32)
    self_update = jnp.zeros((ROWS, DW), jnp.bfloat16).at[target].set(self_rows, mode='drop')
    cross_update = jnp.zeros((ROWS, DW), jnp.bfloat16).at[target].set(cross_rows, mode='drop')
    new_cache = jnp.zeros((ROWS, HIST, KVH, 2 * HD), jnp.bfloat16).at[target].set(written, mode='drop')
    return (self_update, cross_update, new_cache)
```

```python
import functools
import math

import jax
import jax.numpy as jnp
from jax import lax
from jax.experimental import pallas as pl
from jax.experimental.pallas import tpu as pltpu
from jax.sharding import PartitionSpec as P

very_low = -1e30


def pack_kernel(devices, rows_here, page_count, per_pair, table, lengths, offset, rank, pool, new_kv, *rest):
    written = rest[0]
    sends = rest[1 : 1 + devices]
    held, in_sem, token_sem, out_sem, send_sem = rest[1 + devices :]

    def page_copy(r, p):
        return pltpu.make_async_copy(pool.at[table[r, p]], held.at[r, p], in_sem.at[r, p])

    def token_copy(r):
        page_len = held.shape[2]
        at = lengths[r]
        return pltpu.make_async_copy(
            new_kv.at[r], held.at[r, at // page_len, at % page_len], token_sem.at[r]
        )

    def out_copy(r):
        return pltpu.make_async_copy(held.at[r], written.at[r], out_sem.at[r])

    @pl.loop(0, rows_here)
    def _(r):
        for p in range(page_count):
            page_copy(r, p).start()

    @pl.loop(0, rows_here)
    def _(r):
        for p in range(page_count):
            page_copy(r, p).wait()
        token_copy(r).start()

    @pl.loop(0, rows_here)
    def _(r):
        token_copy(r).wait()
        out_copy(r).start()
        for d in range(devices):

            @pl.when(offset[r] == d)
            def _():
                pltpu.make_async_copy(held.at[r], sends[d].at[rank[r]], send_sem.at[r]).start()

    @pl.loop(0, rows_here)
    def _(r):
        out_copy(r).wait()

        @pl.when(offset[r] >= 0)
        def _():
            pltpu.make_async_copy(held.at[r], sends[0].at[0], send_sem.at[r]).wait()


def pack(table, lengths, offset, rank, pool, new_kv, devices, per_pair):
    rows_here, page_count = table.shape
    block = (page_count,) + pool.shape[1:]
    anywhere = pl.BlockSpec(memory_space=pl.ANY)
    scalar = pl.BlockSpec(memory_space=pltpu.SMEM)
    moved = 3 * rows_here * math.prod(block) * 2
    return pl.pallas_call(
        functools.partial(pack_kernel, devices, rows_here, page_count, per_pair),
        out_shape=[jax.ShapeDtypeStruct((rows_here,) + block, pool.dtype)]
        + [jax.ShapeDtypeStruct((per_pair,) + block, pool.dtype)] * devices,
        in_specs=[scalar] * 4 + [anywhere] * 2,
        out_specs=[anywhere] * (1 + devices),
        scratch_shapes=[
            pltpu.VMEM((rows_here,) + block, pool.dtype),
            pltpu.SemaphoreType.DMA((rows_here, page_count)),
            pltpu.SemaphoreType.DMA((rows_here,)),
            pltpu.SemaphoreType.DMA((rows_here,)),
            pltpu.SemaphoreType.DMA((rows_here,)),
        ],
        cost_estimate=pl.CostEstimate(flops=0, bytes_accessed=moved, transcendentals=0),
        compiler_params=pltpu.CompilerParams(vmem_limit_bytes=24 << 20),
    )(table, lengths, offset, rank, pool, new_kv)


def settle_kernel(devices, rows_here, offset, rank, *rest):
    arrived = rest[:devices]
    out, held, in_sem, out_sem = rest[devices:]

    @pl.loop(0, rows_here)
    def _(s):
        for d in range(devices):

            @pl.when(offset[s] == d)
            def _():
                pltpu.make_async_copy(arrived[d].at[rank[s]], held.at[s], in_sem.at[s]).start()

        @pl.when(offset[s] < 0)
        def _():
            held[s] = jnp.zeros(held.shape[1:], held.dtype)

    def out_copy(s):
        return pltpu.make_async_copy(held.at[s], out.at[s], out_sem.at[s])

    @pl.loop(0, rows_here)
    def _(s):
        @pl.when(offset[s] >= 0)
        def _():
            pltpu.make_async_copy(arrived[0].at[0], held.at[s], in_sem.at[s]).wait()

        out_copy(s).start()

    @pl.loop(0, rows_here)
    def _(s):
        out_copy(s).wait()


def settle(offset, rank, arrived):
    devices = len(arrived)
    rows_here = offset.shape[0]
    block = arrived[0].shape[1:]
    anywhere = pl.BlockSpec(memory_space=pl.ANY)
    scalar = pl.BlockSpec(memory_space=pltpu.SMEM)
    return pl.pallas_call(
        functools.partial(settle_kernel, devices, rows_here),
        out_shape=jax.ShapeDtypeStruct((rows_here,) + block, arrived[0].dtype),
        in_specs=[scalar] * 2 + [anywhere] * devices,
        out_specs=anywhere,
        scratch_shapes=[
            pltpu.VMEM((rows_here,) + block, arrived[0].dtype),
            pltpu.SemaphoreType.DMA((rows_here,)),
            pltpu.SemaphoreType.DMA((rows_here,)),
        ],
        cost_estimate=pl.CostEstimate(
            flops=0, bytes_accessed=4 * rows_here * math.prod(block), transcendentals=0
        ),
        compiler_params=pltpu.CompilerParams(vmem_limit_bytes=24 << 20),
    )(offset, rank, *arrived)


def self_attend(queries, rows_kv, lengths):
    count_rows, history, kv_heads, width = rows_kv.shape
    head_width = width // 2
    flat = rows_kv.reshape(count_rows, history * kv_heads, width)
    grouped = queries.reshape(count_rows, -1, head_width)
    heads = grouped.shape[1]
    scores = jnp.einsum(
        "nhd,nud->nhu", grouped, flat[..., :head_width], preferred_element_type=jnp.float32
    ) * (1.0 / math.sqrt(head_width))
    shape = (heads, history * kv_heads)
    place = lax.broadcasted_iota(jnp.int32, shape, 1)
    own = (place % kv_heads) == lax.broadcasted_iota(jnp.int32, shape, 0) // (heads // kv_heads)
    seen = own[None] & ((place // kv_heads)[None] <= lengths[:, None, None])
    scores = jnp.where(seen, scores, very_low)
    highest = jnp.max(scores, axis=-1, keepdims=True)
    weights = jnp.exp(scores - highest)
    weight_sum = jnp.sum(weights, axis=-1)
    blended = jnp.einsum(
        "nhu,nud->nhd", weights, flat[..., head_width:], preferred_element_type=jnp.float32
    )
    return (blended / weight_sum[..., None]).reshape(count_rows, -1).astype(jnp.bfloat16)


def cross_attend(cross_query, image_cache, image_of, devices):
    rows_here = cross_query.shape[0]
    rows_all = image_of.shape[0]
    images, tokens, kv_heads, width = image_cache.shape
    head_width = width // 2
    group = rows_all // images
    asked = lax.all_gather(cross_query, "rows", axis=0, tiled=True)
    same = image_of[:, None] == image_of[None, :]
    before = lax.broadcasted_iota(jnp.int32, same.shape, 1) < lax.broadcasted_iota(
        jnp.int32, same.shape, 0
    )
    place = image_of * group + jnp.sum((same & before).astype(jnp.int32), axis=1)
    sort = (lax.broadcasted_iota(jnp.int32, same.shape, 0) == place[None, :]).astype(jnp.bfloat16)
    asked = jnp.dot(sort, asked, preferred_element_type=jnp.float32).astype(jnp.bfloat16)
    asked = asked.reshape(images, group, kv_heads, -1, head_width)
    scores = jnp.einsum(
        "irkgd,inkd->ikrgn", asked, image_cache[..., :head_width], preferred_element_type=jnp.float32
    ) * (1.0 / math.sqrt(head_width))
    highest = jnp.max(scores, axis=-1)
    weights = jnp.exp(scores - highest[..., None])
    weight_sum = jnp.sum(weights, axis=-1)
    blended = jnp.einsum(
        "ikrgn,inkd->irkgd", weights, image_cache[..., head_width:], preferred_element_type=jnp.float32
    )
    highest = highest.transpose(0, 2, 1, 3)
    weight_sum = weight_sum.transpose(0, 2, 1, 3)
    part = (blended / weight_sum[..., None]).astype(jnp.bfloat16).reshape(rows_all, -1)
    part = jnp.dot(sort.T, part, preferred_element_type=jnp.float32).astype(jnp.bfloat16)
    stats = jnp.concatenate(
        [highest.reshape(rows_all, -1), weight_sum.reshape(rows_all, -1)], axis=1
    )[place]
    part = lax.all_to_all(
        part.reshape(devices, rows_here, -1), "rows", split_axis=0, concat_axis=0, tiled=True
    )
    stats = lax.all_to_all(
        stats.reshape(devices, rows_here, -1), "rows", split_axis=0, concat_axis=0, tiled=True
    )
    heads = stats.shape[-1] // 2
    highest, weight_sum = stats[..., :heads], stats[..., heads:]
    share = weight_sum * jnp.exp(highest - jnp.max(highest, axis=0, keepdims=True))
    share = share / jnp.sum(share, axis=0, keepdims=True)
    part = part.reshape(devices, rows_here, heads, head_width).astype(jnp.float32)
    return jnp.sum(part * share[..., None], axis=0).reshape(rows_here, -1).astype(jnp.bfloat16)


def per_device(
    stream,
    self_query,
    new_kv,
    cache_pool,
    page_table,
    lengths,
    migration,
    image_of,
    cross_query,
    image_cache,
    self_output,
    cross_output,
    cross_gate,
):
    rows_here = migration.shape[0]
    devices = lax.axis_size("rows")
    me = lax.axis_index("rows")
    per_pair = max(2, 2 * rows_here // devices)
    page_count = page_table.shape[1]
    page_len, kv_heads, width = cache_pool.shape[1:]
    history = page_count * page_len

    moves = lax.all_gather(migration, "rows", axis=0, tiled=True)
    target_dev = migration[:, 0]
    earlier = (target_dev[:, None] == target_dev[None, :]) & (
        lax.broadcasted_iota(jnp.int32, (rows_here, rows_here), 1)
        < lax.broadcasted_iota(jnp.int32, (rows_here, rows_here), 0)
    )
    rank_here = jnp.sum(earlier.astype(jnp.int32), axis=1)
    offset_here = jnp.where(target_dev >= 0, (target_dev - me + devices) % devices, -1)
    packed = pack(
        page_table, lengths, offset_here, rank_here, cache_pool, new_kv, devices, per_pair
    )
    written, blocks = packed[0], packed[1:]

    def shifted(block, d):
        return lax.ppermute(block, "rows", [(r, (r + d) % devices) for r in range(devices)])

    always = (devices // 2, 1)
    arrived = {0: blocks[0]}
    for d in always:
        arrived[d] = shifted(blocks[d], d)

    rows_all = moves.shape[0]
    to_all, slot_all = moves[:, 0], moves[:, 1]
    number = lax.broadcasted_iota(jnp.int32, (rows_all,), 0)
    source = number // rows_here
    offset_all = jnp.where(to_all >= 0, (to_all - source + devices) % devices, -1)
    first = lax.broadcasted_iota(jnp.int32, (rows_all, rows_all), 0)
    second = lax.broadcasted_iota(jnp.int32, (rows_all, rows_all), 1)
    sooner = (
        (to_all[:, None] == to_all[None, :])
        & (source[:, None] == source[None, :])
        & (second < first)
    )
    rank_all = jnp.sum(sooner.astype(jnp.int32), axis=1)
    slots = lax.broadcasted_iota(jnp.int32, (rows_here, rows_all), 0)
    chosen = (slot_all[None, :] == slots) & (to_all[None, :] == me)
    named = jnp.any(chosen, axis=1)
    slot_offset = jnp.where(named, jnp.sum(jnp.where(chosen, offset_all[None], 0), axis=1), -1)
    slot_rank = jnp.sum(jnp.where(chosen, rank_all[None], 0), axis=1)

    cross_here = cross_attend(cross_query, image_cache, image_of, devices)
    attended_here = self_attend(
        self_query, written.reshape(rows_here, history, kv_heads, width), lengths
    )
    self_part = jnp.dot(attended_here, self_output, preferred_element_type=jnp.float32)
    cross_part = jnp.dot(cross_here, cross_output, preferred_element_type=jnp.float32)
    both = lax.psum_scatter(
        jnp.concatenate([self_part, cross_part], axis=0), "heads", scatter_dimension=1, tiled=True
    )
    self_rows = (stream.astype(jnp.float32) + both[:rows_here]).astype(jnp.bfloat16)
    cross_rows = (jnp.tanh(cross_gate[0]) * both[rows_here:]).astype(jnp.bfloat16)
    finished = lax.all_gather(
        jnp.concatenate([self_rows, cross_rows], axis=1), "rows", axis=0, tiled=True
    )
    updates = jnp.dot(
        chosen.astype(jnp.bfloat16), finished, preferred_element_type=jnp.float32
    ).astype(jnp.bfloat16)
    columns = stream.shape[1]

    others = [d for d in range(1, devices) if d not in always]
    held_back = lax.optimization_barrier(([blocks[d] for d in others], updates))
    updates = held_back[1]
    for d, block in zip(others, held_back[0]):
        arrived[d] = lax.cond(
            jnp.any(offset_all == d), functools.partial(shifted, d=d), lambda b: b, block
        )
    new_cache = settle(slot_offset, slot_rank, [arrived[d] for d in range(devices)])
    return (
        updates[:, :columns],
        updates[:, columns:],
        new_cache.reshape(rows_here, history, kv_heads, width),
    )


def solution(mesh):
    in_specs = (
        P("rows", "heads"),
        P("rows", "heads"),
        P("rows", "heads", None),
        P("rows", None, "heads", None),
        P("rows", None),
        P("rows"),
        P("rows", None),
        P(),
        P("rows", "heads"),
        P(None, "rows", "heads", None),
        P("heads", None),
        P("heads", None),
        P(),
    )
    out_specs = (P("rows", "heads"), P("rows", "heads"), P("rows", None, "heads", None))
    return jax.shard_map(
        per_device, mesh=mesh, in_specs=in_specs, out_specs=out_specs, check_vma=False
    )
```

```python
import functools
import math

import jax
import jax.numpy as jnp
from jax import lax
from jax.experimental import pallas as pl
from jax.experimental.pallas import tpu as pltpu
from jax.sharding import PartitionSpec as P

very_low = -1e30


def pack_kernel(devices, rows_here, page_count, per_pair, table, lengths, offset, rank, pool, new_kv, *rest):
    written = rest[0]
    sends = rest[1 : 1 + devices]
    held, in_sem, token_sem, out_sem, send_sem = rest[1 + devices :]

    def page_copy(r, p):
        return pltpu.make_async_copy(pool.at[table[r, p]], held.at[r, p], in_sem.at[r, p])

    def token_copy(r):
        page_len = held.shape[2]
        at = lengths[r]
        return pltpu.make_async_copy(
            new_kv.at[r], held.at[r, at // page_len, at % page_len], token_sem.at[r]
        )

    def out_copy(r):
        return pltpu.make_async_copy(held.at[r], written.at[r], out_sem.at[r])

    @pl.loop(0, rows_here)
    def _(r):
        for p in range(page_count):
            page_copy(r, p).start()

    @pl.loop(0, rows_here)
    def _(r):
        for p in range(page_count):
            page_copy(r, p).wait()
        token_copy(r).start()

    @pl.loop(0, rows_here)
    def _(r):
        token_copy(r).wait()
        out_copy(r).start()
        for d in range(devices):

            @pl.when(offset[r] == d)
            def _():
                pltpu.make_async_copy(held.at[r], sends[d].at[rank[r]], send_sem.at[r]).start()

    @pl.loop(0, rows_here)
    def _(r):
        out_copy(r).wait()

        @pl.when(offset[r] >= 0)
        def _():
            pltpu.make_async_copy(held.at[r], sends[0].at[0], send_sem.at[r]).wait()


def pack(table, lengths, offset, rank, pool, new_kv, devices, per_pair):
    rows_here, page_count = table.shape
    block = (page_count,) + pool.shape[1:]
    anywhere = pl.BlockSpec(memory_space=pl.ANY)
    scalar = pl.BlockSpec(memory_space=pltpu.SMEM)
    moved = 3 * rows_here * math.prod(block) * 2
    return pl.pallas_call(
        functools.partial(pack_kernel, devices, rows_here, page_count, per_pair),
        out_shape=[jax.ShapeDtypeStruct((rows_here,) + block, pool.dtype)]
        + [jax.ShapeDtypeStruct((per_pair,) + block, pool.dtype)] * devices,
        in_specs=[scalar] * 4 + [anywhere] * 2,
        out_specs=[anywhere] * (1 + devices),
        scratch_shapes=[
            pltpu.VMEM((rows_here,) + block, pool.dtype),
            pltpu.SemaphoreType.DMA((rows_here, page_count)),
            pltpu.SemaphoreType.DMA((rows_here,)),
            pltpu.SemaphoreType.DMA((rows_here,)),
            pltpu.SemaphoreType.DMA((rows_here,)),
        ],
        cost_estimate=pl.CostEstimate(flops=0, bytes_accessed=moved, transcendentals=0),
        compiler_params=pltpu.CompilerParams(vmem_limit_bytes=60 << 20),
    )(table, lengths, offset, rank, pool, new_kv)


def settle_kernel(devices, rows_here, offset, rank, *rest):
    arrived = rest[:devices]
    out, held, in_sem, out_sem = rest[devices:]

    @pl.loop(0, rows_here)
    def _(s):
        for d in range(devices):

            @pl.when(offset[s] == d)
            def _():
                pltpu.make_async_copy(arrived[d].at[rank[s]], held.at[s], in_sem.at[s]).start()

        @pl.when(offset[s] < 0)
        def _():
            held[s] = jnp.zeros(held.shape[1:], held.dtype)

    def out_copy(s):
        return pltpu.make_async_copy(held.at[s], out.at[s], out_sem.at[s])

    @pl.loop(0, rows_here)
    def _(s):
        @pl.when(offset[s] >= 0)
        def _():
            pltpu.make_async_copy(arrived[0].at[0], held.at[s], in_sem.at[s]).wait()

        out_copy(s).start()

    @pl.loop(0, rows_here)
    def _(s):
        out_copy(s).wait()


def settle(offset, rank, arrived):
    devices = len(arrived)
    rows_here = offset.shape[0]
    block = arrived[0].shape[1:]
    anywhere = pl.BlockSpec(memory_space=pl.ANY)
    scalar = pl.BlockSpec(memory_space=pltpu.SMEM)
    return pl.pallas_call(
        functools.partial(settle_kernel, devices, rows_here),
        out_shape=jax.ShapeDtypeStruct((rows_here,) + block, arrived[0].dtype),
        in_specs=[scalar] * 2 + [anywhere] * devices,
        out_specs=anywhere,
        scratch_shapes=[
            pltpu.VMEM((rows_here,) + block, arrived[0].dtype),
            pltpu.SemaphoreType.DMA((rows_here,)),
            pltpu.SemaphoreType.DMA((rows_here,)),
        ],
        cost_estimate=pl.CostEstimate(
            flops=0, bytes_accessed=4 * rows_here * math.prod(block), transcendentals=0
        ),
        compiler_params=pltpu.CompilerParams(vmem_limit_bytes=60 << 20),
    )(offset, rank, *arrived)


def exchange_kernel(axis, devices, gather, count, *refs):
    sources, landed = refs[:count], refs[count : 2 * count]
    send_sem, recv_sem, own_sem = refs[2 * count :]
    me = lax.axis_index(axis)
    barrier = pltpu.get_barrier_semaphore()
    for k in range(1, devices):
        pl.semaphore_signal(
            barrier,
            inc=1,
            device_id={axis: lax.rem(me + k, devices)},
            device_id_type=pl.DeviceIdType.MESH,
        )
    pl.semaphore_wait(barrier, devices - 1)

    def out_of(i, peer):
        return sources[i] if gather else sources[i].at[peer]

    def copy(i, k, slot):
        peer = lax.rem(me + k, devices)
        return pltpu.make_async_remote_copy(
            src_ref=out_of(i, peer),
            dst_ref=landed[i].at[slot],
            send_sem=send_sem.at[k, i],
            recv_sem=recv_sem.at[k, i],
            device_id={axis: peer},
            device_id_type=pl.DeviceIdType.MESH,
        )

    for k in range(1, devices):
        for i in range(count):
            copy(i, k, me).start()
    for i in range(count):
        pltpu.make_async_copy(out_of(i, me), landed[i].at[me], own_sem.at[i]).start()
    for i in range(count):
        pltpu.make_async_copy(out_of(i, me), landed[i].at[me], own_sem.at[i]).wait()
    for k in range(1, devices):
        for i in range(count):
            copy(i, k, me).wait_send()
            copy(i, k, lax.rem(me - k + devices, devices)).wait_recv()


def exchange(axis, number, arrays, gather=False):
    devices = lax.axis_size(axis)
    count = len(arrays)
    in_vmem = pl.BlockSpec(memory_space=pltpu.VMEM)
    return pl.pallas_call(
        functools.partial(exchange_kernel, axis, devices, gather, count),
        out_shape=[
            jax.ShapeDtypeStruct(((devices,) if gather else ()) + a.shape, a.dtype) for a in arrays
        ],
        in_specs=[in_vmem] * count,
        out_specs=[in_vmem] * count,
        scratch_shapes=[
            pltpu.SemaphoreType.DMA((devices, count)),
            pltpu.SemaphoreType.DMA((devices, count)),
            pltpu.SemaphoreType.DMA((count,)),
        ],
        compiler_params=pltpu.CompilerParams(collective_id=number, has_side_effects=True),
    )(*arrays)


def widened(array):
    return jnp.pad(array, ((0, 0), (0, -array.shape[1] % 128)))


def self_attend(queries, rows_kv, lengths):
    count_rows, history, kv_heads, width = rows_kv.shape
    head_width = width // 2
    flat = rows_kv.reshape(count_rows, history * kv_heads, width)
    grouped = queries.reshape(count_rows, -1, head_width)
    heads = grouped.shape[1]
    scores = jnp.einsum(
        "nhd,nud->nhu", grouped, flat[..., :head_width], preferred_element_type=jnp.float32
    ) * (1.0 / math.sqrt(head_width))
    shape = (heads, history * kv_heads)
    place = lax.broadcasted_iota(jnp.int32, shape, 1)
    own = (place % kv_heads) == lax.broadcasted_iota(jnp.int32, shape, 0) // (heads // kv_heads)
    seen = own[None] & ((place // kv_heads)[None] <= lengths[:, None, None])
    scores = jnp.where(seen, scores, very_low)
    highest = jnp.max(scores, axis=-1, keepdims=True)
    weights = jnp.exp(scores - highest)
    weight_sum = jnp.sum(weights, axis=-1)
    blended = jnp.einsum(
        "nhu,nud->nhd", weights, flat[..., head_width:], preferred_element_type=jnp.float32
    )
    return (blended / weight_sum[..., None]).reshape(count_rows, -1).astype(jnp.bfloat16)


def cross_parts(asked, image_cache, image_of, devices):
    rows_here = asked.shape[0] // devices
    rows_all = image_of.shape[0]
    images, tokens, kv_heads, width = image_cache.shape
    head_width = width // 2
    group = rows_all // images
    same = image_of[:, None] == image_of[None, :]
    before = lax.broadcasted_iota(jnp.int32, same.shape, 1) < lax.broadcasted_iota(
        jnp.int32, same.shape, 0
    )
    place = image_of * group + jnp.sum((same & before).astype(jnp.int32), axis=1)
    sort = (lax.broadcasted_iota(jnp.int32, same.shape, 0) == place[None, :]).astype(jnp.bfloat16)
    asked = jnp.dot(sort, asked, preferred_element_type=jnp.float32).astype(jnp.bfloat16)
    asked = asked.reshape(images, group, kv_heads, -1, head_width)
    scores = jnp.einsum(
        "irkgd,inkd->ikrgn", asked, image_cache[..., :head_width], preferred_element_type=jnp.float32
    ) * (1.0 / math.sqrt(head_width))
    highest = jnp.max(scores, axis=-1)
    weights = jnp.exp(scores - highest[..., None])
    weight_sum = jnp.sum(weights, axis=-1)
    blended = jnp.einsum(
        "ikrgn,inkd->irkgd", weights, image_cache[..., head_width:], preferred_element_type=jnp.float32
    )
    highest = highest.transpose(0, 2, 1, 3)
    weight_sum = weight_sum.transpose(0, 2, 1, 3)
    part = (blended / weight_sum[..., None]).astype(jnp.bfloat16).reshape(rows_all, -1)
    part = jnp.dot(sort.T, part, preferred_element_type=jnp.float32).astype(jnp.bfloat16)
    stats = jnp.concatenate(
        [highest.reshape(rows_all, -1), weight_sum.reshape(rows_all, -1)], axis=1
    )[place]
    return exchange(
        "rows",
        2,
        [part.reshape(devices, rows_here, -1), widened(stats).reshape(devices, rows_here, -1)],
    )


def cross_blend(part, stats, head_width):
    devices, rows_here, width = part.shape
    heads = width // head_width
    highest, weight_sum = stats[..., :heads], stats[..., heads : 2 * heads]
    share = weight_sum * jnp.exp(highest - jnp.max(highest, axis=0, keepdims=True))
    share = share / jnp.sum(share, axis=0, keepdims=True)
    part = part.reshape(devices, rows_here, heads, head_width).astype(jnp.float32)
    return jnp.sum(part * share[..., None], axis=0).reshape(rows_here, -1).astype(jnp.bfloat16)


def per_device(
    stream,
    self_query,
    new_kv,
    cache_pool,
    page_table,
    lengths,
    migration,
    image_of,
    cross_query,
    image_cache,
    self_output,
    cross_output,
    cross_gate,
):
    rows_here = migration.shape[0]
    devices = lax.axis_size("rows")
    me = lax.axis_index("rows")
    per_pair = max(2, 2 * rows_here // devices)
    page_count = page_table.shape[1]
    page_len, kv_heads, width = cache_pool.shape[1:]
    history = page_count * page_len

    asked, moves = exchange("rows", 1, [cross_query, widened(migration)], gather=True)
    asked = asked.reshape(devices * rows_here, -1)
    moves = moves.reshape(devices * rows_here, -1)[:, :2]
    part, stats = cross_parts(asked, image_cache, image_of, devices)
    target_dev = migration[:, 0]
    earlier = (target_dev[:, None] == target_dev[None, :]) & (
        lax.broadcasted_iota(jnp.int32, (rows_here, rows_here), 1)
        < lax.broadcasted_iota(jnp.int32, (rows_here, rows_here), 0)
    )
    rank_here = jnp.sum(earlier.astype(jnp.int32), axis=1)
    offset_here = jnp.where(target_dev >= 0, (target_dev - me + devices) % devices, -1)
    packed = pack(
        page_table, lengths, offset_here, rank_here, cache_pool, new_kv, devices, per_pair
    )
    packed, part, stats = lax.optimization_barrier((packed, part, stats))
    written, blocks = packed[0], packed[1:]

    def shifted(block, d):
        return lax.ppermute(block, "rows", [(r, (r + d) % devices) for r in range(devices)])

    always = (devices // 2, 1)
    arrived = {0: blocks[0]}
    for d in always:
        arrived[d] = shifted(blocks[d], d)

    rows_all = moves.shape[0]
    to_all, slot_all = moves[:, 0], moves[:, 1]
    number = lax.broadcasted_iota(jnp.int32, (rows_all,), 0)
    source = number // rows_here
    offset_all = jnp.where(to_all >= 0, (to_all - source + devices) % devices, -1)
    first = lax.broadcasted_iota(jnp.int32, (rows_all, rows_all), 0)
    second = lax.broadcasted_iota(jnp.int32, (rows_all, rows_all), 1)
    sooner = (
        (to_all[:, None] == to_all[None, :])
        & (source[:, None] == source[None, :])
        & (second < first)
    )
    rank_all = jnp.sum(sooner.astype(jnp.int32), axis=1)
    slots = lax.broadcasted_iota(jnp.int32, (rows_here, rows_all), 0)
    chosen = (slot_all[None, :] == slots) & (to_all[None, :] == me)
    named = jnp.any(chosen, axis=1)
    slot_offset = jnp.where(named, jnp.sum(jnp.where(chosen, offset_all[None], 0), axis=1), -1)
    slot_rank = jnp.sum(jnp.where(chosen, rank_all[None], 0), axis=1)

    cross_here = cross_blend(part, stats, width // 2)
    attended_here = self_attend(
        self_query, written.reshape(rows_here, history, kv_heads, width), lengths
    )
    self_part = jnp.dot(attended_here, self_output, preferred_element_type=jnp.float32)
    cross_part = jnp.dot(cross_here, cross_output, preferred_element_type=jnp.float32)
    both = jnp.concatenate([self_part, cross_part], axis=0)
    shares = lax.axis_size("heads")
    columns = stream.shape[1]
    both = both.reshape(2 * rows_here, shares, columns).transpose(1, 0, 2)
    both = jnp.sum(exchange("heads", 3, [both])[0], axis=0)
    self_rows = (stream.astype(jnp.float32) + both[:rows_here]).astype(jnp.bfloat16)
    cross_rows = (jnp.tanh(cross_gate[0]) * both[rows_here:]).astype(jnp.bfloat16)
    finished = jnp.concatenate([self_rows, cross_rows], axis=1)

    others = [d for d in range(1, devices) if d not in always]
    held_back, finished = lax.optimization_barrier(([blocks[d] for d in others], finished))
    for d, block in zip(others, held_back):
        arrived[d] = lax.cond(
            jnp.any(offset_all == d), functools.partial(shifted, d=d), lambda b: b, block
        )
    arrived, finished = lax.optimization_barrier((arrived, finished))
    place = jnp.where(target_dev >= 0, target_dev * per_pair + rank_here, -1)
    leaving = lax.broadcasted_iota(jnp.int32, (devices * per_pair, rows_here), 0) == place[None, :]
    finished = jnp.dot(
        leaving.astype(jnp.bfloat16), finished, preferred_element_type=jnp.float32
    ).astype(jnp.bfloat16)
    finished = exchange("rows", 4, [finished.reshape(devices, per_pair, -1)])[0]
    came = (me - slot_offset + devices) % devices * per_pair + slot_rank
    came = jnp.where(slot_offset >= 0, came, -1)
    entering = lax.broadcasted_iota(jnp.int32, (rows_here, devices * per_pair), 1) == came[:, None]
    updates = jnp.dot(
        entering.astype(jnp.bfloat16),
        finished.reshape(devices * per_pair, -1),
        preferred_element_type=jnp.float32,
    ).astype(jnp.bfloat16)
    new_cache = settle(slot_offset, slot_rank, [arrived[d] for d in range(devices)])
    return (
        updates[:, :columns],
        updates[:, columns:],
        new_cache.reshape(rows_here, history, kv_heads, width),
    )


def solution(mesh):
    in_specs = (
        P("rows", "heads"),
        P("rows", "heads"),
        P("rows", "heads", None),
        P("rows", None, "heads", None),
        P("rows", None),
        P("rows"),
        P("rows", None),
        P(),
        P("rows", "heads"),
        P(None, "rows", "heads", None),
        P("heads", None),
        P("heads", None),
        P(),
    )
    out_specs = (P("rows", "heads"), P("rows", "heads"), P("rows", None, "heads", None))
    return jax.shard_map(
        per_device, mesh=mesh, in_specs=in_specs, out_specs=out_specs, check_vma=False
    )
```

```python
import functools
import itertools
import math

import jax
import jax.numpy as jnp
from jax import lax
from jax.experimental import pallas as pl
from jax.experimental.pallas import tpu as pltpu
from jax.sharding import PartitionSpec as P

very_low = -1e30


def pack_kernel(devices, rows_here, page_count, per_pair, table, lengths, offset, rank, pool, new_kv, *rest):
    written = rest[0]
    sends = rest[1 : 1 + devices]
    held, in_sem, token_sem, out_sem, send_sem = rest[1 + devices :]

    def page_copy(r, p):
        return pltpu.make_async_copy(pool.at[table[r, p]], held.at[r, p], in_sem.at[r, p])

    def token_copy(r):
        page_len = held.shape[2]
        at = lengths[r]
        return pltpu.make_async_copy(
            new_kv.at[r], held.at[r, at // page_len, at % page_len], token_sem.at[r]
        )

    def out_copy(r):
        return pltpu.make_async_copy(held.at[r], written.at[r], out_sem.at[r])

    @pl.loop(0, rows_here)
    def _(r):
        for p in range(page_count):
            page_copy(r, p).start()

    @pl.loop(0, rows_here)
    def _(r):
        for p in range(page_count):
            page_copy(r, p).wait()
        token_copy(r).start()

    @pl.loop(0, rows_here)
    def _(r):
        token_copy(r).wait()
        out_copy(r).start()
        for d in range(devices):

            @pl.when(offset[r] == d)
            def _():
                pltpu.make_async_copy(held.at[r], sends[d].at[rank[r]], send_sem.at[r]).start()

    @pl.loop(0, rows_here)
    def _(r):
        out_copy(r).wait()

        @pl.when(offset[r] >= 0)
        def _():
            pltpu.make_async_copy(held.at[r], sends[0].at[0], send_sem.at[r]).wait()


def pack(table, lengths, offset, rank, pool, new_kv, devices, per_pair):
    rows_here, page_count = table.shape
    block = (page_count,) + pool.shape[1:]
    anywhere = pl.BlockSpec(memory_space=pl.ANY)
    scalar = pl.BlockSpec(memory_space=pltpu.SMEM)
    moved = 3 * rows_here * math.prod(block) * 2
    return pl.pallas_call(
        functools.partial(pack_kernel, devices, rows_here, page_count, per_pair),
        out_shape=[jax.ShapeDtypeStruct((rows_here,) + block, pool.dtype)]
        + [jax.ShapeDtypeStruct((per_pair,) + block, pool.dtype)] * devices,
        in_specs=[scalar] * 4 + [anywhere] * 2,
        out_specs=[anywhere] * (1 + devices),
        scratch_shapes=[
            pltpu.VMEM((rows_here,) + block, pool.dtype),
            pltpu.SemaphoreType.DMA((rows_here, page_count)),
            pltpu.SemaphoreType.DMA((rows_here,)),
            pltpu.SemaphoreType.DMA((rows_here,)),
            pltpu.SemaphoreType.DMA((rows_here,)),
        ],
        cost_estimate=pl.CostEstimate(flops=0, bytes_accessed=moved, transcendentals=0),
        compiler_params=pltpu.CompilerParams(vmem_limit_bytes=60 << 20),
    )(table, lengths, offset, rank, pool, new_kv)


def settle_kernel(devices, rows_here, offset, rank, *rest):
    arrived = rest[:devices]
    out, held, in_sem, out_sem = rest[devices:]

    @pl.loop(0, rows_here)
    def _(s):
        for d in range(devices):

            @pl.when(offset[s] == d)
            def _():
                pltpu.make_async_copy(arrived[d].at[rank[s]], held.at[s], in_sem.at[s]).start()

        @pl.when(offset[s] < 0)
        def _():
            held[s] = jnp.zeros(held.shape[1:], held.dtype)

    def out_copy(s):
        return pltpu.make_async_copy(held.at[s], out.at[s], out_sem.at[s])

    @pl.loop(0, rows_here)
    def _(s):
        @pl.when(offset[s] >= 0)
        def _():
            pltpu.make_async_copy(arrived[0].at[0], held.at[s], in_sem.at[s]).wait()

        out_copy(s).start()

    @pl.loop(0, rows_here)
    def _(s):
        out_copy(s).wait()


def settle(offset, rank, arrived):
    devices = len(arrived)
    rows_here = offset.shape[0]
    block = arrived[0].shape[1:]
    anywhere = pl.BlockSpec(memory_space=pl.ANY)
    scalar = pl.BlockSpec(memory_space=pltpu.SMEM)
    return pl.pallas_call(
        functools.partial(settle_kernel, devices, rows_here),
        out_shape=jax.ShapeDtypeStruct((rows_here,) + block, arrived[0].dtype),
        in_specs=[scalar] * 2 + [anywhere] * devices,
        out_specs=anywhere,
        scratch_shapes=[
            pltpu.VMEM((rows_here,) + block, arrived[0].dtype),
            pltpu.SemaphoreType.DMA((rows_here,)),
            pltpu.SemaphoreType.DMA((rows_here,)),
        ],
        cost_estimate=pl.CostEstimate(
            flops=0, bytes_accessed=4 * rows_here * math.prod(block), transcendentals=0
        ),
        compiler_params=pltpu.CompilerParams(vmem_limit_bytes=60 << 20),
    )(offset, rank, *arrived)


def exchange_kernel(axis, devices, gather, count, *refs):
    sources, landed = refs[:count], refs[count : 2 * count]
    send_sem, recv_sem, own_sem = refs[2 * count :]
    me = lax.axis_index(axis)
    barrier = pltpu.get_barrier_semaphore()
    for k in range(1, devices):
        pl.semaphore_signal(
            barrier,
            inc=1,
            device_id={axis: lax.rem(me + k, devices)},
            device_id_type=pl.DeviceIdType.MESH,
        )
    pl.semaphore_wait(barrier, devices - 1)

    def out_of(i, peer):
        return sources[i] if gather else sources[i].at[peer]

    def copy(i, k, slot):
        peer = lax.rem(me + k, devices)
        return pltpu.make_async_remote_copy(
            src_ref=out_of(i, peer),
            dst_ref=landed[i].at[slot],
            send_sem=send_sem.at[k, i],
            recv_sem=recv_sem.at[k, i],
            device_id={axis: peer},
            device_id_type=pl.DeviceIdType.MESH,
        )

    for k in range(1, devices):
        for i in range(count):
            copy(i, k, me).start()
    for i in range(count):
        pltpu.make_async_copy(out_of(i, me), landed[i].at[me], own_sem.at[i]).start()
    for i in range(count):
        pltpu.make_async_copy(out_of(i, me), landed[i].at[me], own_sem.at[i]).wait()
    for k in range(1, devices):
        for i in range(count):
            copy(i, k, me).wait_send()
            copy(i, k, lax.rem(me - k + devices, devices)).wait_recv()


def exchange(axis, number, arrays, gather=False):
    devices = lax.axis_size(axis)
    count = len(arrays)
    in_vmem = pl.BlockSpec(memory_space=pltpu.VMEM)
    return pl.pallas_call(
        functools.partial(exchange_kernel, axis, devices, gather, count),
        out_shape=[
            jax.ShapeDtypeStruct(((devices,) if gather else ()) + a.shape, a.dtype) for a in arrays
        ],
        in_specs=[in_vmem] * count,
        out_specs=[in_vmem] * count,
        scratch_shapes=[
            pltpu.SemaphoreType.DMA((devices, count)),
            pltpu.SemaphoreType.DMA((devices, count)),
            pltpu.SemaphoreType.DMA((count,)),
        ],
        compiler_params=pltpu.CompilerParams(collective_id=number, has_side_effects=True),
    )(*arrays)


def widened(array):
    return jnp.pad(array, ((0, 0), (0, -array.shape[1] % 128)))


def self_attend(queries, rows_kv, lengths):
    count_rows, history, kv_heads, width = rows_kv.shape
    head_width = width // 2
    flat = rows_kv.reshape(count_rows, history * kv_heads, width)
    grouped = queries.reshape(count_rows, -1, head_width)
    heads = grouped.shape[1]
    scores = jnp.einsum(
        "nhd,nud->nhu", grouped, flat[..., :head_width], preferred_element_type=jnp.float32
    ) * (1.0 / math.sqrt(head_width))
    shape = (heads, history * kv_heads)
    place = lax.broadcasted_iota(jnp.int32, shape, 1)
    own = (place % kv_heads) == lax.broadcasted_iota(jnp.int32, shape, 0) // (heads // kv_heads)
    seen = own[None] & ((place // kv_heads)[None] <= lengths[:, None, None])
    scores = jnp.where(seen, scores, very_low)
    highest = jnp.max(scores, axis=-1, keepdims=True)
    weights = jnp.exp(scores - highest)
    weight_sum = jnp.sum(weights, axis=-1)
    blended = jnp.einsum(
        "nhu,nud->nhd", weights, flat[..., head_width:], preferred_element_type=jnp.float32
    )
    return (blended / weight_sum[..., None]).reshape(count_rows, -1).astype(jnp.bfloat16)


def cross_parts(asked, image_cache, image_of, devices):
    rows_here = asked.shape[0] // devices
    rows_all = image_of.shape[0]
    images, tokens, kv_heads, width = image_cache.shape
    head_width = width // 2
    group = rows_all // images
    same = image_of[:, None] == image_of[None, :]
    before = lax.broadcasted_iota(jnp.int32, same.shape, 1) < lax.broadcasted_iota(
        jnp.int32, same.shape, 0
    )
    place = image_of * group + jnp.sum((same & before).astype(jnp.int32), axis=1)
    sort = (lax.broadcasted_iota(jnp.int32, same.shape, 0) == place[None, :]).astype(jnp.bfloat16)
    asked = jnp.dot(sort, asked, preferred_element_type=jnp.float32).astype(jnp.bfloat16)
    asked = asked.reshape(images, group, kv_heads, -1, head_width)
    scores = jnp.einsum(
        "irkgd,inkd->ikrgn", asked, image_cache[..., :head_width], preferred_element_type=jnp.float32
    ) * (1.0 / math.sqrt(head_width))
    highest = jnp.max(scores, axis=-1)
    weights = jnp.exp(scores - highest[..., None])
    weight_sum = jnp.sum(weights, axis=-1)
    blended = jnp.einsum(
        "ikrgn,inkd->irkgd", weights, image_cache[..., head_width:], preferred_element_type=jnp.float32
    )
    highest = highest.transpose(0, 2, 1, 3)
    weight_sum = weight_sum.transpose(0, 2, 1, 3)
    part = (blended / weight_sum[..., None]).astype(jnp.bfloat16).reshape(rows_all, -1)
    part = jnp.dot(sort.T, part, preferred_element_type=jnp.float32).astype(jnp.bfloat16)
    stats = jnp.concatenate(
        [highest.reshape(rows_all, -1), weight_sum.reshape(rows_all, -1)], axis=1
    )[place]
    return exchange(
        "rows",
        2,
        [part.reshape(devices, rows_here, -1), widened(stats).reshape(devices, rows_here, -1)],
    )


def cross_blend(part, stats, head_width):
    devices, rows_here, width = part.shape
    heads = width // head_width
    highest, weight_sum = stats[..., :heads], stats[..., heads : 2 * heads]
    share = weight_sum * jnp.exp(highest - jnp.max(highest, axis=0, keepdims=True))
    share = share / jnp.sum(share, axis=0, keepdims=True)
    part = part.reshape(devices, rows_here, heads, head_width).astype(jnp.float32)
    return jnp.sum(part * share[..., None], axis=0).reshape(rows_here, -1).astype(jnp.bfloat16)


def per_device(
    stream,
    self_query,
    new_kv,
    cache_pool,
    page_table,
    lengths,
    migration,
    image_of,
    cross_query,
    image_cache,
    self_output,
    cross_output,
    cross_gate,
):
    rows_here = migration.shape[0]
    devices = lax.axis_size("rows")
    me = lax.axis_index("rows")
    per_pair = max(2, 2 * rows_here // devices)
    page_count = page_table.shape[1]
    page_len, kv_heads, width = cache_pool.shape[1:]
    history = page_count * page_len

    asked, moves = exchange("rows", 1, [cross_query, widened(migration)], gather=True)
    asked = asked.reshape(devices * rows_here, -1)
    moves = moves.reshape(devices * rows_here, -1)[:, :2]
    part, stats = cross_parts(asked, image_cache, image_of, devices)
    target_dev = migration[:, 0]
    earlier = (target_dev[:, None] == target_dev[None, :]) & (
        lax.broadcasted_iota(jnp.int32, (rows_here, rows_here), 1)
        < lax.broadcasted_iota(jnp.int32, (rows_here, rows_here), 0)
    )
    rank_here = jnp.sum(earlier.astype(jnp.int32), axis=1)
    offset_here = jnp.where(target_dev >= 0, (target_dev - me + devices) % devices, -1)
    packed = pack(
        page_table, lengths, offset_here, rank_here, cache_pool, new_kv, devices, per_pair
    )
    packed, part, stats = lax.optimization_barrier((packed, part, stats))
    written, blocks = packed[0], packed[1:]

    def shifted(block, d):
        return lax.ppermute(block, "rows", [(r, (r + d) % devices) for r in range(devices)])

    always = (devices // 2, 1)
    arrived = {0: blocks[0]}
    for d in always:
        arrived[d] = shifted(blocks[d], d)

    rows_all = moves.shape[0]
    to_all, slot_all = moves[:, 0], moves[:, 1]
    number = lax.broadcasted_iota(jnp.int32, (rows_all,), 0)
    source = number // rows_here
    offset_all = jnp.where(to_all >= 0, (to_all - source + devices) % devices, -1)
    first = lax.broadcasted_iota(jnp.int32, (rows_all, rows_all), 0)
    second = lax.broadcasted_iota(jnp.int32, (rows_all, rows_all), 1)
    sooner = (
        (to_all[:, None] == to_all[None, :])
        & (source[:, None] == source[None, :])
        & (second < first)
    )
    rank_all = jnp.sum(sooner.astype(jnp.int32), axis=1)
    slots = lax.broadcasted_iota(jnp.int32, (rows_here, rows_all), 0)
    chosen = (slot_all[None, :] == slots) & (to_all[None, :] == me)
    named = jnp.any(chosen, axis=1)
    slot_offset = jnp.where(named, jnp.sum(jnp.where(chosen, offset_all[None], 0), axis=1), -1)
    slot_rank = jnp.sum(jnp.where(chosen, rank_all[None], 0), axis=1)

    cross_here = cross_blend(part, stats, width // 2)
    attended_here = self_attend(
        self_query, written.reshape(rows_here, history, kv_heads, width), lengths
    )
    self_part = jnp.dot(attended_here, self_output, preferred_element_type=jnp.float32)
    cross_part = jnp.dot(cross_here, cross_output, preferred_element_type=jnp.float32)
    both = jnp.concatenate([self_part, cross_part], axis=0)
    shares = lax.axis_size("heads")
    columns = stream.shape[1]
    both = both.reshape(2 * rows_here, shares, columns).transpose(1, 0, 2)
    both = jnp.sum(exchange("heads", 3, [both])[0], axis=0)
    self_rows = (stream.astype(jnp.float32) + both[:rows_here]).astype(jnp.bfloat16)
    cross_rows = (jnp.tanh(cross_gate[0]) * both[rows_here:]).astype(jnp.bfloat16)
    finished = jnp.concatenate([self_rows, cross_rows], axis=1)

    others = [d for d in range(1, devices) if d not in always]
    few = [set(c) for size in range(3) for c in itertools.combinations(others, size)]
    if len(few) > 32:
        few = []
    in_use = jnp.stack([jnp.any(offset_all == d) for d in others]).astype(jnp.int32)
    code = jnp.int32(len(few))
    for i, subset in enumerate(few):
        wanted = jnp.array([int(d in subset) for d in others], jnp.int32)
        code = jnp.where(jnp.all(in_use == wanted), i, code)

    held_back, finished = lax.optimization_barrier(([blocks[d] for d in others], finished))

    def branch(subset):
        def run(*held):
            return [
                shifted(b, d) if d in subset else b for d, b in zip(others, held)
            ]

        return run

    results = lax.switch(code, [branch(c) for c in few + [set(others)]], *held_back)
    arrived.update(zip(others, results))
    arrived, finished = lax.optimization_barrier((arrived, finished))
    place = jnp.where(target_dev >= 0, target_dev * per_pair + rank_here, -1)
    leaving = lax.broadcasted_iota(jnp.int32, (devices * per_pair, rows_here), 0) == place[None, :]
    finished = jnp.dot(
        leaving.astype(jnp.bfloat16), finished, preferred_element_type=jnp.float32
    ).astype(jnp.bfloat16)
    finished = exchange("rows", 4, [finished.reshape(devices, per_pair, -1)])[0]
    came = (me - slot_offset + devices) % devices * per_pair + slot_rank
    came = jnp.where(slot_offset >= 0, came, -1)
    entering = lax.broadcasted_iota(jnp.int32, (rows_here, devices * per_pair), 1) == came[:, None]
    updates = jnp.dot(
        entering.astype(jnp.bfloat16),
        finished.reshape(devices * per_pair, -1),
        preferred_element_type=jnp.float32,
    ).astype(jnp.bfloat16)
    new_cache = settle(slot_offset, slot_rank, [arrived[d] for d in range(devices)])
    return (
        updates[:, :columns],
        updates[:, columns:],
        new_cache.reshape(rows_here, history, kv_heads, width),
    )


def solution(mesh):
    in_specs = (
        P("rows", "heads"),
        P("rows", "heads"),
        P("rows", "heads", None),
        P("rows", None, "heads", None),
        P("rows", None),
        P("rows"),
        P("rows", None),
        P(),
        P("rows", "heads"),
        P(None, "rows", "heads", None),
        P("heads", None),
        P("heads", None),
        P(),
    )
    out_specs = (P("rows", "heads"), P("rows", "heads"), P("rows", None, "heads", None))
    return jax.shard_map(
        per_device, mesh=mesh, in_specs=in_specs, out_specs=out_specs, check_vma=False
    )
```

```python
import functools
import itertools
import math

import jax
import jax.numpy as jnp
from jax import lax
from jax.experimental import pallas as pl
from jax.experimental.pallas import tpu as pltpu
from jax.sharding import PartitionSpec as P

very_low = -1e30


def pack_kernel(devices, rows_here, page_count, per_pair, table, lengths, offset, rank, pool, new_kv, *rest):
    written = rest[0]
    sends = rest[1 : 1 + devices]
    held, in_sem, token_sem, out_sem, send_sem = rest[1 + devices :]

    def page_copy(r, p):
        return pltpu.make_async_copy(pool.at[table[r, p]], held.at[r, p], in_sem.at[r, p])

    def token_copy(r):
        page_len = held.shape[2]
        at = lengths[r]
        return pltpu.make_async_copy(
            new_kv.at[r], held.at[r, at // page_len, at % page_len], token_sem.at[r]
        )

    def out_copy(r):
        return pltpu.make_async_copy(held.at[r], written.at[r], out_sem.at[r])

    @pl.loop(0, rows_here)
    def _(r):
        for p in range(page_count):
            page_copy(r, p).start()

    @pl.loop(0, rows_here)
    def _(r):
        for p in range(page_count):
            page_copy(r, p).wait()
        token_copy(r).start()

    @pl.loop(0, rows_here)
    def _(r):
        token_copy(r).wait()
        out_copy(r).start()
        for d in range(devices):

            @pl.when(offset[r] == d)
            def _():
                pltpu.make_async_copy(held.at[r], sends[d].at[rank[r]], send_sem.at[r]).start()

    @pl.loop(0, rows_here)
    def _(r):
        out_copy(r).wait()

        @pl.when(offset[r] >= 0)
        def _():
            pltpu.make_async_copy(held.at[r], sends[0].at[0], send_sem.at[r]).wait()


def pack(table, lengths, offset, rank, pool, new_kv, devices, per_pair):
    rows_here, page_count = table.shape
    block = (page_count,) + pool.shape[1:]
    anywhere = pl.BlockSpec(memory_space=pl.ANY)
    scalar = pl.BlockSpec(memory_space=pltpu.SMEM)
    moved = 3 * rows_here * math.prod(block) * 2
    return pl.pallas_call(
        functools.partial(pack_kernel, devices, rows_here, page_count, per_pair),
        out_shape=[jax.ShapeDtypeStruct((rows_here,) + block, pool.dtype)]
        + [jax.ShapeDtypeStruct((per_pair,) + block, pool.dtype)] * devices,
        in_specs=[scalar] * 4 + [anywhere] * 2,
        out_specs=[anywhere] * (1 + devices),
        scratch_shapes=[
            pltpu.VMEM((rows_here,) + block, pool.dtype),
            pltpu.SemaphoreType.DMA((rows_here, page_count)),
            pltpu.SemaphoreType.DMA((rows_here,)),
            pltpu.SemaphoreType.DMA((rows_here,)),
            pltpu.SemaphoreType.DMA((rows_here,)),
        ],
        cost_estimate=pl.CostEstimate(flops=0, bytes_accessed=moved, transcendentals=0),
        compiler_params=pltpu.CompilerParams(vmem_limit_bytes=60 << 20),
    )(table, lengths, offset, rank, pool, new_kv)


def settle_kernel(devices, rows_here, offset, rank, *rest):
    arrived = rest[:devices]
    out, held, in_sem, out_sem = rest[devices:]

    @pl.loop(0, rows_here)
    def _(s):
        for d in range(devices):

            @pl.when(offset[s] == d)
            def _():
                pltpu.make_async_copy(arrived[d].at[rank[s]], held.at[s], in_sem.at[s]).start()

        @pl.when(offset[s] < 0)
        def _():
            held[s] = jnp.zeros(held.shape[1:], held.dtype)

    def out_copy(s):
        return pltpu.make_async_copy(held.at[s], out.at[s], out_sem.at[s])

    @pl.loop(0, rows_here)
    def _(s):
        @pl.when(offset[s] >= 0)
        def _():
            pltpu.make_async_copy(arrived[0].at[0], held.at[s], in_sem.at[s]).wait()

        out_copy(s).start()

    @pl.loop(0, rows_here)
    def _(s):
        out_copy(s).wait()


def settle(offset, rank, arrived):
    devices = len(arrived)
    rows_here = offset.shape[0]
    block = arrived[0].shape[1:]
    anywhere = pl.BlockSpec(memory_space=pl.ANY)
    scalar = pl.BlockSpec(memory_space=pltpu.SMEM)
    return pl.pallas_call(
        functools.partial(settle_kernel, devices, rows_here),
        out_shape=jax.ShapeDtypeStruct((rows_here,) + block, arrived[0].dtype),
        in_specs=[scalar] * 2 + [anywhere] * devices,
        out_specs=anywhere,
        scratch_shapes=[
            pltpu.VMEM((rows_here,) + block, arrived[0].dtype),
            pltpu.SemaphoreType.DMA((rows_here,)),
            pltpu.SemaphoreType.DMA((rows_here,)),
        ],
        cost_estimate=pl.CostEstimate(
            flops=0, bytes_accessed=4 * rows_here * math.prod(block), transcendentals=0
        ),
        compiler_params=pltpu.CompilerParams(vmem_limit_bytes=60 << 20),
    )(offset, rank, *arrived)


def exchange_kernel(axis, devices, count, *refs):
    sources, landed = refs[:count], refs[count : 2 * count]
    send_sem, recv_sem, own_sem = refs[2 * count :]
    me = lax.axis_index(axis)
    barrier = pltpu.get_barrier_semaphore()
    for k in range(1, devices):
        pl.semaphore_signal(
            barrier,
            inc=1,
            device_id={axis: lax.rem(me + k, devices)},
            device_id_type=pl.DeviceIdType.MESH,
        )
    pl.semaphore_wait(barrier, devices - 1)

    def out_of(i, peer):
        return sources[i].at[peer]

    def copy(i, k, slot):
        peer = lax.rem(me + k, devices)
        return pltpu.make_async_remote_copy(
            src_ref=out_of(i, peer),
            dst_ref=landed[i].at[slot],
            send_sem=send_sem.at[k, i],
            recv_sem=recv_sem.at[k, i],
            device_id={axis: peer},
            device_id_type=pl.DeviceIdType.MESH,
        )

    for k in range(1, devices):
        for i in range(count):
            copy(i, k, me).start()
    for i in range(count):
        pltpu.make_async_copy(out_of(i, me), landed[i].at[me], own_sem.at[i]).start()
    for i in range(count):
        pltpu.make_async_copy(out_of(i, me), landed[i].at[me], own_sem.at[i]).wait()
    for k in range(1, devices):
        for i in range(count):
            copy(i, k, me).wait_send()
            copy(i, k, lax.rem(me - k + devices, devices)).wait_recv()


def gather_kernel(axis, devices, columns, count, *refs):
    sources, landed = refs[:count], refs[count : 2 * count]
    send_sem, recv_sem, own_sem = refs[2 * count :]
    me = lax.axis_index(axis)
    levels = devices // columns
    level, column = lax.div(me, columns), lax.rem(me, columns)

    def up(k):
        return lax.rem(level + k, levels) * columns + column

    def across(k):
        return level * columns + lax.rem(column + k, columns)

    barrier = pltpu.get_barrier_semaphore()
    partners = [up(k) for k in range(1, levels)] + [across(k) for k in range(1, columns)]
    for peer in partners:
        pl.semaphore_signal(
            barrier, inc=1, device_id={axis: peer}, device_id_type=pl.DeviceIdType.MESH
        )
    pl.semaphore_wait(barrier, len(partners))

    def copy(i, kz, kx):
        owner = me if kx == 0 else up(levels - kz)
        return pltpu.make_async_remote_copy(
            src_ref=sources[i] if kx == 0 or kz == 0 else landed[i].at[owner],
            dst_ref=landed[i].at[owner],
            send_sem=send_sem.at[kz * columns + kx, i],
            recv_sem=recv_sem.at[kz * columns + kx, i],
            device_id={axis: up(kz) if kx == 0 else across(kx)},
            device_id_type=pl.DeviceIdType.MESH,
        )

    def arrival(i, kz, kx):
        owner = lax.rem(level + levels - kz, levels) * columns + lax.rem(
            column + columns - kx, columns
        )
        return pltpu.make_async_remote_copy(
            src_ref=sources[i],
            dst_ref=landed[i].at[owner],
            send_sem=send_sem.at[kz * columns + kx, i],
            recv_sem=recv_sem.at[kz * columns + kx, i],
            device_id={axis: up(kz) if kx == 0 else across(kx)},
            device_id_type=pl.DeviceIdType.MESH,
        )

    every = range(count)
    for kz in range(1, levels):
        for i in every:
            copy(i, kz, 0).start()
    for kx in range(1, columns):
        for i in every:
            copy(i, 0, kx).start()
    for i in every:
        pltpu.make_async_copy(sources[i], landed[i].at[me], own_sem.at[i]).start()
    for kz in range(1, levels):
        for i in every:
            arrival(i, kz, 0).wait_recv()
            for kx in range(1, columns):
                copy(i, kz, kx).start()
    for i in every:
        pltpu.make_async_copy(sources[i], landed[i].at[me], own_sem.at[i]).wait()
    for kz in range(levels):
        for kx in range(columns):
            if kz or kx:
                for i in every:
                    copy(i, kz, kx).wait_send()
                    if kx:
                        arrival(i, kz, kx).wait_recv()


def exchange(axis, number, arrays, columns=0):
    devices = lax.axis_size(axis)
    count = len(arrays)
    gather = columns > 0
    in_vmem = pl.BlockSpec(memory_space=pltpu.VMEM)
    if gather:
        body = functools.partial(gather_kernel, axis, devices, columns, count)
    else:
        body = functools.partial(exchange_kernel, axis, devices, count)
    return pl.pallas_call(
        body,
        out_shape=[
            jax.ShapeDtypeStruct(((devices,) if gather else ()) + a.shape, a.dtype) for a in arrays
        ],
        in_specs=[in_vmem] * count,
        out_specs=[in_vmem] * count,
        scratch_shapes=[
            pltpu.SemaphoreType.DMA((devices, count)),
            pltpu.SemaphoreType.DMA((devices, count)),
            pltpu.SemaphoreType.DMA((count,)),
        ],
        compiler_params=pltpu.CompilerParams(collective_id=number, has_side_effects=True),
    )(*arrays)


def widened(array):
    return jnp.pad(array, ((0, 0), (0, -array.shape[1] % 128)))


def self_attend(queries, rows_kv, lengths):
    count_rows, history, kv_heads, width = rows_kv.shape
    head_width = width // 2
    flat = rows_kv.reshape(count_rows, history * kv_heads, width)
    grouped = queries.reshape(count_rows, -1, head_width)
    heads = grouped.shape[1]
    scores = jnp.einsum(
        "nhd,nud->nhu", grouped, flat[..., :head_width], preferred_element_type=jnp.float32
    ) * (1.0 / math.sqrt(head_width))
    shape = (heads, history * kv_heads)
    place = lax.broadcasted_iota(jnp.int32, shape, 1)
    own = (place % kv_heads) == lax.broadcasted_iota(jnp.int32, shape, 0) // (heads // kv_heads)
    seen = own[None] & ((place // kv_heads)[None] <= lengths[:, None, None])
    scores = jnp.where(seen, scores, very_low)
    highest = jnp.max(scores, axis=-1, keepdims=True)
    weights = jnp.exp(scores - highest)
    weight_sum = jnp.sum(weights, axis=-1)
    blended = jnp.einsum(
        "nhu,nud->nhd", weights, flat[..., head_width:], preferred_element_type=jnp.float32
    )
    return (blended / weight_sum[..., None]).reshape(count_rows, -1).astype(jnp.bfloat16)


def cross_parts(asked, image_cache, image_of, devices):
    rows_here = asked.shape[0] // devices
    rows_all = image_of.shape[0]
    images, tokens, kv_heads, width = image_cache.shape
    head_width = width // 2
    group = rows_all // images
    same = image_of[:, None] == image_of[None, :]
    before = lax.broadcasted_iota(jnp.int32, same.shape, 1) < lax.broadcasted_iota(
        jnp.int32, same.shape, 0
    )
    place = image_of * group + jnp.sum((same & before).astype(jnp.int32), axis=1)
    sort = (lax.broadcasted_iota(jnp.int32, same.shape, 0) == place[None, :]).astype(jnp.bfloat16)
    asked = jnp.dot(sort, asked, preferred_element_type=jnp.float32).astype(jnp.bfloat16)
    asked = asked.reshape(images, group, kv_heads, -1, head_width)
    scores = jnp.einsum(
        "irkgd,inkd->ikrgn", asked, image_cache[..., :head_width], preferred_element_type=jnp.float32
    ) * (1.0 / math.sqrt(head_width))
    highest = jnp.max(scores, axis=-1)
    weights = jnp.exp(scores - highest[..., None])
    weight_sum = jnp.sum(weights, axis=-1)
    blended = jnp.einsum(
        "ikrgn,inkd->irkgd", weights, image_cache[..., head_width:], preferred_element_type=jnp.float32
    )
    highest = highest.transpose(0, 2, 1, 3)
    weight_sum = weight_sum.transpose(0, 2, 1, 3)
    part = (blended / weight_sum[..., None]).astype(jnp.bfloat16).reshape(rows_all, -1)
    part = jnp.dot(sort.T, part, preferred_element_type=jnp.float32).astype(jnp.bfloat16)
    stats = jnp.concatenate(
        [highest.reshape(rows_all, -1), weight_sum.reshape(rows_all, -1)], axis=1
    )[place]
    return exchange(
        "rows",
        2,
        [part.reshape(devices, rows_here, -1), widened(stats).reshape(devices, rows_here, -1)],
    )


def cross_blend(part, stats, head_width):
    devices, rows_here, width = part.shape
    heads = width // head_width
    highest, weight_sum = stats[..., :heads], stats[..., heads : 2 * heads]
    share = weight_sum * jnp.exp(highest - jnp.max(highest, axis=0, keepdims=True))
    share = share / jnp.sum(share, axis=0, keepdims=True)
    part = part.reshape(devices, rows_here, heads, head_width).astype(jnp.float32)
    return jnp.sum(part * share[..., None], axis=0).reshape(rows_here, -1).astype(jnp.bfloat16)


def per_device(
    stream,
    self_query,
    new_kv,
    cache_pool,
    page_table,
    lengths,
    migration,
    image_of,
    cross_query,
    image_cache,
    self_output,
    cross_output,
    cross_gate,
):
    rows_here = migration.shape[0]
    devices = lax.axis_size("rows")
    columns = max(1, lax.axis_size("heads") // 2)
    columns = columns if devices % columns == 0 else 1
    me = lax.axis_index("rows")
    per_pair = max(2, 2 * rows_here // devices)
    page_count = page_table.shape[1]
    page_len, kv_heads, width = cache_pool.shape[1:]
    history = page_count * page_len

    asked, moves = exchange("rows", 1, [cross_query, widened(migration)], columns)
    asked = asked.reshape(devices * rows_here, -1)
    moves = moves.reshape(devices * rows_here, -1)[:, :2]
    part, stats = cross_parts(asked, image_cache, image_of, devices)
    target_dev = migration[:, 0]
    earlier = (target_dev[:, None] == target_dev[None, :]) & (
        lax.broadcasted_iota(jnp.int32, (rows_here, rows_here), 1)
        < lax.broadcasted_iota(jnp.int32, (rows_here, rows_here), 0)
    )
    rank_here = jnp.sum(earlier.astype(jnp.int32), axis=1)
    offset_here = jnp.where(target_dev >= 0, (target_dev - me + devices) % devices, -1)
    packed = pack(
        page_table, lengths, offset_here, rank_here, cache_pool, new_kv, devices, per_pair
    )
    packed, part, stats = lax.optimization_barrier((packed, part, stats))
    written, blocks = packed[0], packed[1:]

    def shifted(block, d):
        return lax.ppermute(block, "rows", [(r, (r + d) % devices) for r in range(devices)])

    def crossed(block, d):
        there = [(r + d) % devices for r in range(devices)]
        between = [r // columns * columns + t % columns for r, t in enumerate(there)]
        block = lax.ppermute(block, "rows", list(enumerate(between)))
        return lax.ppermute(block, "rows", list(zip(between, there)))

    always = (devices // 2, 1)
    arrived = {0: blocks[0]}
    for d in always:
        arrived[d] = shifted(blocks[d], d)

    rows_all = moves.shape[0]
    to_all, slot_all = moves[:, 0], moves[:, 1]
    number = lax.broadcasted_iota(jnp.int32, (rows_all,), 0)
    source = number // rows_here
    offset_all = jnp.where(to_all >= 0, (to_all - source + devices) % devices, -1)
    first = lax.broadcasted_iota(jnp.int32, (rows_all, rows_all), 0)
    second = lax.broadcasted_iota(jnp.int32, (rows_all, rows_all), 1)
    sooner = (
        (to_all[:, None] == to_all[None, :])
        & (source[:, None] == source[None, :])
        & (second < first)
    )
    rank_all = jnp.sum(sooner.astype(jnp.int32), axis=1)
    slots = lax.broadcasted_iota(jnp.int32, (rows_here, rows_all), 0)
    chosen = (slot_all[None, :] == slots) & (to_all[None, :] == me)
    named = jnp.any(chosen, axis=1)
    slot_offset = jnp.where(named, jnp.sum(jnp.where(chosen, offset_all[None], 0), axis=1), -1)
    slot_rank = jnp.sum(jnp.where(chosen, rank_all[None], 0), axis=1)

    cross_here = cross_blend(part, stats, width // 2)
    attended_here = self_attend(
        self_query, written.reshape(rows_here, history, kv_heads, width), lengths
    )
    self_part = jnp.dot(attended_here, self_output, preferred_element_type=jnp.float32)
    cross_part = jnp.dot(cross_here, cross_output, preferred_element_type=jnp.float32)
    both = jnp.concatenate([self_part, cross_part], axis=0)
    shares = lax.axis_size("heads")
    width_here = stream.shape[1]
    both = both.reshape(2 * rows_here, shares, width_here).transpose(1, 0, 2)
    both = jnp.sum(exchange("heads", 3, [both])[0], axis=0)
    self_rows = (stream.astype(jnp.float32) + both[:rows_here]).astype(jnp.bfloat16)
    cross_rows = (jnp.tanh(cross_gate[0]) * both[rows_here:]).astype(jnp.bfloat16)
    finished = jnp.concatenate([self_rows, cross_rows], axis=1)
    place = jnp.where(target_dev >= 0, target_dev * per_pair + rank_here, -1)
    leaving = lax.broadcasted_iota(jnp.int32, (devices * per_pair, rows_here), 0) == place[None, :]
    finished = jnp.dot(
        leaving.astype(jnp.bfloat16), finished, preferred_element_type=jnp.float32
    ).astype(jnp.bfloat16)

    others = [d for d in range(1, devices) if d not in always]
    few = [set(c) for size in range(3) for c in itertools.combinations(others, size)]
    if len(few) > 32:
        few = []
    in_use = jnp.stack([jnp.any(offset_all == d) for d in others]).astype(jnp.int32)
    code = jnp.int32(len(few))
    for i, subset in enumerate(few):
        wanted = jnp.array([int(d in subset) for d in others], jnp.int32)
        code = jnp.where(jnp.all(in_use == wanted), i, code)

    held_back, finished = lax.optimization_barrier(([blocks[d] for d in others], finished))

    def branch(subset):
        odd = [d for d in subset if d % columns]

        def moved(b, d):
            if d not in subset:
                return b
            return crossed(b, d) if odd == [1 + columns] == [d] else shifted(b, d)

        def run(*held):
            return [moved(b, d) for d, b in zip(others, held)]

        return run

    results = lax.switch(code, [branch(c) for c in few + [set(others)]], *held_back)
    arrived.update(zip(others, results))
    arrived, finished = lax.optimization_barrier((arrived, finished))
    finished = exchange("rows", 4, [finished.reshape(devices, per_pair, -1)])[0]
    came = (me - slot_offset + devices) % devices * per_pair + slot_rank
    came = jnp.where(slot_offset >= 0, came, -1)
    entering = lax.broadcasted_iota(jnp.int32, (rows_here, devices * per_pair), 1) == came[:, None]
    updates = jnp.dot(
        entering.astype(jnp.bfloat16),
        finished.reshape(devices * per_pair, -1),
        preferred_element_type=jnp.float32,
    ).astype(jnp.bfloat16)
    new_cache = settle(slot_offset, slot_rank, [arrived[d] for d in range(devices)])
    return (
        updates[:, :width_here],
        updates[:, width_here:],
        new_cache.reshape(rows_here, history, kv_heads, width),
    )


def solution(mesh):
    in_specs = (
        P("rows", "heads"),
        P("rows", "heads"),
        P("rows", "heads", None),
        P("rows", None, "heads", None),
        P("rows", None),
        P("rows"),
        P("rows", None),
        P(),
        P("rows", "heads"),
        P(None, "rows", "heads", None),
        P("heads", None),
        P("heads", None),
        P(),
    )
    out_specs = (P("rows", "heads"), P("rows", "heads"), P("rows", None, "heads", None))
    return jax.shard_map(
        per_device, mesh=mesh, in_specs=in_specs, out_specs=out_specs, check_vma=False
    )
```
